32 devices in a mesh: dp: 4 (over y, x), tensor: 8 (over z, core).
Axes of the slice: x: 2, y: 2, z: 4, core: 2. Of those that a mesh axis runs over, the one named last changes fastest.
Arguments:
- inputs: bfloat16 [8192, 1024], P(('dp', 'tensor')), may hold values from -6 to 6
- project: bfloat16 [3, 1024, 1024], P(None, None, 'tensor'), may hold values from -0.25 to 0.25
- offsets: float32 [2, 1024], P(None, 'tensor'), may hold values from -3 to 3
- combine: bfloat16 [1024, 1024], P('tensor'), may hold values from -0.75 to 0.75
- combine_bias: float32 [1024], replicated, may hold values from -2 to 2
- norm_gain: float32 [2, 1024], replicated, may hold values from 0.25 to 1.75
- norm_shift: float32 [2, 1024], replicated, may hold values from -2 to 2
- expand: bfloat16 [1024, 4096], P(None, 'tensor'), may hold values from -0.1875 to 0.1875
- expand_bias: float32 [4096], P('tensor'), may hold values from -3 to 3
- contract: bfloat16 [4096, 1024], P('tensor'), may hold values from -0.09375 to 0.09375
- contract_bias: float32 [1024], replicated, may hold values from -2 to 2
- cotangent: bfloat16 [8192, 1024], P(('dp', 'tensor')), may hold values from -16 to 16
Outputs:
- block_out: bfloat16 [8192, 1024], P(('dp', 'tensor'))
- input_grad: bfloat16 [8192, 1024], P(('dp', 'tensor'))
- project_grad: float32 [3, 1024, 1024], P(None, None, 'tensor')
- offset_grad: float32 [2, 1024], P(None, 'tensor')
- combine_grad: float32 [1024, 1024], P('tensor')
- mixing_grad: float32 [1024], replicated
- gain_grad: float32 [2, 1024], replicated
- shift_grad: float32 [2, 1024], replicated
- expand_grad: float32 [1024, 4096], P(None, 'tensor')
- widening_grad: float32 [4096], P('tensor')
- contract_grad: float32 [4096, 1024], P('tensor')
- narrowing_grad: float32 [1024], replicated
The draws below stay inside these ranges and needn't reach their ends.
All inputs are finite; a program needn't handle non-finite values.
Results may differ from the reference program's by a relative error of at most 0.02.
Values may be sent and summed in bfloat16 or wider, within the bound.
No kernel may reach another device: no remote copies, remote signals or barrier semaphores. Data moves between devices by JAX's collectives and lax.ppermute only.
A program may use at most 128 MiB of HBM per device.

```python
import math
import jax
import jax.numpy as jnp
from jax import lax

D = 1024
HEADS = 16
FF = 4096
L = 2048
QBLOCK = 512
HEAD_DIM = 64
TOKENS = 8192


def draw_cotangent(key, part):
    position = jnp.arange(TOKENS, dtype=jnp.float32) / (TOKENS - 1)
    base = jnp.clip(jax.random.normal(key, (TOKENS, D), jnp.float32), -6.0, 6.0)
    ramp = jnp.exp(position * math.log(3.0)) / 1.7
    values = base * ramp[:, None]
    return values.astype(jnp.bfloat16)


def steps_of(stream_key, extent, pieces, low, top_value):
    loudness, own = 1.0, jax.random.fold_in(stream_key, 6)
    for dim, shards_of in pieces:
        steps = jnp.exp(jax.random.uniform(jax.random.fold_in(own, dim), (shards_of,), jnp.float32, low / len(pieces), top_value / len(pieces)))
        loudness = loudness * jnp.repeat(steps, extent[dim] // shards_of).reshape([-1 if axis == dim else 1 for axis in range(len(extent))])
    return loudness


def scatter_about(rng, extent, scale, limit, pieces=(), kind=jnp.bfloat16):
    factor_of = steps_of(rng, extent, pieces, -0.22, 0.18) if pieces else 1.0
    array = jax.random.normal(rng, extent, jnp.float32) * scale * factor_of
    return jnp.minimum(jnp.maximum(array, -limit), limit).astype(kind)


def setup_inputs(seed: int = 0) -> dict:
    key_of = jax.random.split(jax.random.key(seed), 13)
    return {
        "inputs": scatter_about(key_of[0], (TOKENS, D), 1.0, 6.0, ((0, 32),)),
        "project": scatter_about(key_of[1], (3, D, D), (D // 2) ** -0.5, 0.25, ((2, 8),)),
        "offsets": scatter_about(key_of[2], (2, D), 0.5, 3.0, ((1, 8),), jnp.float32),
        "combine": scatter_about(key_of[3], (D, D), (D // 16) ** -0.5, 0.75, ((0, 8),)),
        "combine_bias": scatter_about(key_of[4], (D,), 0.3, 2.0, (), jnp.float32),
        "norm_gain": jnp.clip(1.0 + 0.15 * jax.random.normal(key_of[5], (2, D), jnp.float32), 0.25, 1.75),
        "norm_shift": scatter_about(key_of[6], (2, D), 0.3, 2.0, (), jnp.float32),
        "expand": scatter_about(key_of[7], (D, FF), D ** -0.5, 0.1875, ((1, 8),)),
        "expand_bias": scatter_about(key_of[8], (FF,), 0.5, 3.0, ((0, 8),), jnp.float32),
        "contract": scatter_about(key_of[9], (FF, D), FF ** -0.5, 0.09375, ((0, 8),)),
        "contract_bias": scatter_about(key_of[10], (D,), 0.3, 2.0, (), jnp.float32),
        "cotangent": draw_cotangent(jax.random.fold_in(key_of[12], 71), 0),
    }


HIGHEST = lax.Precision.HIGHEST

@jax.custom_vjp
def low(v):
    return lax.optimization_barrier(v.astype(jnp.bfloat16)).astype(jnp.float32)

@jax.custom_vjp
def low_back(v):
    return v

def low_keep(v):
    return (low(v), None)

def low_pass(kept, grad):
    return (grad,)

def back_keep(v):
    return (v, None)

def back_low(kept, grad):
    return (low(grad),)
low.defvjp(low_keep, low_pass)
low_back.defvjp(back_keep, back_low)

def layer_norm(features, gain_row, shift_row):
    center = features - lax.optimization_barrier(jnp.mean(features, axis=-1, keepdims=True))
    spread = lax.optimization_barrier(jnp.mean(center * center, axis=-1, keepdims=True))
    return center * lax.rsqrt(spread + 1e-06) * gain_row + shift_row

def gelu_exact(values):
    return jax.nn.gelu(values, approximate=False)

def sequence_forward(params, seq_in):
    project, offsets, combine, combine_bias, norm_gain, norm_shift, expand, expand_bias, contract, contract_bias = params
    normed = low(layer_norm(seq_in, norm_gain[0], norm_shift[0]))
    mapped = jnp.einsum('td,kde->kte', normed, project, precision=HIGHEST)
    bias_rows = jnp.stack([offsets[0], jnp.zeros_like(offsets[0]), offsets[1]])
    mapped = low(low_back(mapped + bias_rows[:, None, :]))
    head_split = mapped.reshape(3, L, HEADS, HEAD_DIM)
    queries = head_split[0]
    keys_all = head_split[1]
    values_all = head_split[2]
    scale_factor = 1.0 / math.sqrt(HEAD_DIM)

    def attend_block(query_blk):
        scores = jnp.einsum('qhe,khe->hqk', query_blk, keys_all, precision=HIGHEST) * scale_factor
        scores = low_back(scores)
        weights = low(jax.nn.softmax(scores, axis=-1))
        return jnp.einsum('hqk,khe->qhe', weights, values_all, precision=HIGHEST)
    attended = lax.map(jax.checkpoint(attend_block), queries.reshape(L // QBLOCK, QBLOCK, HEADS, HEAD_DIM))
    attended = low(low_back(attended.reshape(L, D)))
    branch = low_back(jnp.dot(attended, combine, precision=HIGHEST) + combine_bias)
    hidden = seq_in + branch
    normed_two = low(layer_norm(hidden, norm_gain[1], norm_shift[1]))
    before = low_back(jnp.dot(normed_two, expand, precision=HIGHEST) + expand_bias)
    active = low(gelu_exact(before))
    return hidden + jnp.dot(active, contract, precision=HIGHEST) + contract_bias

def add_pair(first, second):
    return first + second

def reference(inputs, project, offsets, combine, combine_bias, norm_gain, norm_shift, expand, expand_bias, contract, contract_bias, cotangent):
    params = tuple((operand.astype(jnp.float32) for operand in (project, offsets, combine, combine_bias, norm_gain, norm_shift, expand, expand_bias, contract, contract_bias)))
    seqs_in = inputs.astype(jnp.float32).reshape(TOKENS // L, L, D)
    seqs_grad = cotangent.astype(jnp.float32).reshape(TOKENS // L, L, D)

    def step_one(totals, pair_items):
        seq_in, seq_grad = pair_items
        result, pullback = jax.vjp(sequence_forward, params, seq_in)
        grad_params, grad_in = pullback(seq_grad)
        totals = jax.tree.map(add_pair, totals, grad_params)
        return (totals, (result.astype(jnp.bfloat16), grad_in.astype(jnp.bfloat16)))
    initial = jax.tree.map(jnp.zeros_like, params)
    totals, (results, grads_in) = lax.scan(step_one, initial, (seqs_in, seqs_grad))
    return (results.reshape(TOKENS, D), grads_in.reshape(TOKENS, D), totals[0], totals[1], totals[2], totals[3], totals[4], totals[5], totals[6], totals[7], totals[8], totals[9])
```

```python
import functools
import math

import jax
import jax.numpy as jnp
from jax import lax
from jax.sharding import PartitionSpec as P

L = 2048
QBLOCK = 512
SEQ_DEV = 1
CORES = 2
HEAD_DIM = 64


def layer_norm(features, gain_row, shift_row):
    center = features - jnp.mean(features, axis=-1, keepdims=True)
    spread = jnp.mean(center * center, axis=-1, keepdims=True)
    return center * lax.rsqrt(spread + 1e-06) * gain_row + shift_row


def gelu_exact(values):
    return jax.nn.gelu(values, approximate=False)


def attend_forward(queries, keys_all, values_all):
    scale_factor = 1.0 / math.sqrt(HEAD_DIM)

    def one_sequence(sequence_items):
        query_seq, key_seq, value_seq = sequence_items
        heads_here = query_seq.shape[1]

        def one_block(query_blk):
            scores = (
                jnp.einsum("qhe,khe->hqk", query_blk, key_seq, preferred_element_type=jnp.float32)
                * scale_factor
            )
            highest = jnp.max(scores, axis=-1, keepdims=True)
            raised = jnp.exp(scores - highest)
            summed = jnp.sum(raised, axis=-1, keepdims=True)
            weights = (raised / summed).astype(jnp.bfloat16)
            result = jnp.einsum(
                "hqk,khe->qhe", weights, value_seq, preferred_element_type=jnp.float32
            )
            return (result.astype(jnp.bfloat16), (highest + jnp.log(summed))[:, :, 0])

        blocks = query_seq.reshape(L // QBLOCK, QBLOCK, heads_here, HEAD_DIM)
        results, log_totals = lax.map(one_block, blocks)
        return (results.reshape(L, heads_here, HEAD_DIM), log_totals)

    return lax.map(one_sequence, (queries, keys_all, values_all))


def attend_backward(queries, keys_all, values_all, grad_out, log_totals):
    scale_factor = 1.0 / math.sqrt(HEAD_DIM)

    def one_sequence(sequence_items):
        query_seq, key_seq, value_seq, grad_seq, total_seq = sequence_items
        heads_here = query_seq.shape[1]
        shape_blocks = (L // QBLOCK, QBLOCK, heads_here, HEAD_DIM)

        def one_block(carried, block_items):
            key_grad, value_grad = carried
            query_blk, grad_blk, total_blk = block_items
            scores = (
                jnp.einsum("qhe,khe->hqk", query_blk, key_seq, preferred_element_type=jnp.float32)
                * scale_factor
            )
            probs = jnp.exp(scores - total_blk[:, :, None])
            grad_probs = jnp.einsum(
                "qhe,khe->hqk", grad_blk, value_seq, preferred_element_type=jnp.float32
            )
            row_dots = jnp.sum(probs * grad_probs, axis=-1, keepdims=True)
            grad_scores = (probs * (grad_probs - row_dots)).astype(jnp.bfloat16)
            query_grad = (
                jnp.einsum("hqk,khe->qhe", grad_scores, key_seq, preferred_element_type=jnp.float32)
                * scale_factor
            )
            key_grad = (
                key_grad
                + jnp.einsum(
                    "hqk,qhe->khe", grad_scores, query_blk, preferred_element_type=jnp.float32
                )
                * scale_factor
            )
            value_grad = value_grad + jnp.einsum(
                "hqk,qhe->khe",
                probs.astype(jnp.bfloat16),
                grad_blk,
                preferred_element_type=jnp.float32,
            )
            return ((key_grad, value_grad), query_grad)

        empty = jnp.zeros((L, heads_here, HEAD_DIM), jnp.float32)
        (key_grad, value_grad), query_grad = lax.scan(
            one_block,
            (empty, empty),
            (query_seq.reshape(shape_blocks), grad_seq.reshape(shape_blocks), total_seq),
        )
        return (query_grad.reshape(L, heads_here, HEAD_DIM), key_grad, value_grad)

    return lax.map(one_sequence, (queries, keys_all, values_all, grad_out, log_totals))


def grid_of(dp):
    nx = 1
    while nx * nx < dp:
        nx *= 2
    return dp // nx, nx


class Plane:
    def __init__(self, dp, tensor):
        self.ny, self.nx = grid_of(dp)
        self.dp, self.tensor = dp, tensor

    def _perm(self, axis, step):
        ny, nx = self.ny, self.nx
        if axis == "x":
            return [(y * nx + x, y * nx + (x + step) % nx) for y in range(ny) for x in range(nx)]
        return [(y * nx + x, (y + step) % ny * nx + x) for y in range(ny) for x in range(nx)]

    def size(self, axis):
        return self.nx if axis == "x" else self.ny

    def swap_cores(self, value):
        return lax.ppermute(value, "tensor", [(t, t ^ 1) for t in range(self.tensor)])

    def gather(self, value, axis):
        parts = [value]
        for _ in range(self.size(axis) - 1):
            parts.append(lax.ppermute(parts[-1], "dp", self._perm(axis, 1)))
        return parts

    def scatter(self, parts, axis):
        total = parts[-1]
        for part in parts[-2::-1]:
            moved = lax.ppermute(total.astype(jnp.bfloat16), "dp", self._perm(axis, -1))
            total = part + moved.astype(jnp.float32)
        return total

    def gather_rows(self, rows):
        half = rows.shape[0] // 2
        first, second = rows[:half], rows[half:]
        by_x = self.gather(first, "x")
        by_y = self.gather(second, "y")
        near = jnp.concatenate(by_x[1:] + by_y[1:])
        far_first = self.gather(jnp.concatenate(by_x), "y")[1:]
        far_second = self.gather(jnp.concatenate(by_y), "x")[1:]
        far = jnp.concatenate(far_first + far_second)
        return [jnp.concatenate([part, self.swap_cores(part)]) for part in (rows, near, far)]

    def scatter_rows(self, chunks):
        own, near, far = [self._fold(chunk) for chunk in chunks]
        half = own.shape[0] // 2
        size_x, size_y = half * self.nx, half * self.ny
        split = size_x * (self.ny - 1)
        far_first = [far[k * size_x : (k + 1) * size_x] for k in range(self.ny - 1)]
        far_second = [far[split + k * size_y : split + (k + 1) * size_y] for k in range(self.nx - 1)]
        near_first, near_second = near[: size_x - half], near[size_x - half :]
        first = self.scatter([jnp.concatenate([own[:half], near_first])] + far_first, "y")
        second = self.scatter([jnp.concatenate([own[half:], near_second])] + far_second, "x")
        first = self.scatter([first[k * half : (k + 1) * half] for k in range(self.nx)], "x")
        second = self.scatter([second[k * half : (k + 1) * half] for k in range(self.ny)], "y")
        return jnp.concatenate([first, second])

    def _fold(self, chunk):
        half = chunk.shape[0] // 2
        return chunk[:half].astype(jnp.float32) + self.swap_cores(chunk[half:]).astype(jnp.float32)

    def sum_dp(self, value):
        half = value.shape[0] // 2
        halves = []
        for part, axes in ((value[:half], "xy"), (value[half:], "yx")):
            for axis in axes:
                gathered = self.gather(part, axis)
                total = sum(item.astype(jnp.float32) for item in gathered)
                part = total.astype(jnp.bfloat16)
            halves.append(total)
        return jnp.concatenate(halves)

    def gather_dp(self, value):
        half = value.shape[0] // 2
        first = self.gather(value[:half], "x")
        second = self.gather(value[half:], "y")
        first = self.gather(jnp.stack(first), "y")
        second = self.gather(jnp.stack(second), "x")
        me = lax.axis_index("dp")
        my_y, my_x = me // self.nx, me % self.nx
        out = jnp.zeros((self.dp,) + value.shape, value.dtype)
        for far in range(self.ny):
            for near in range(self.nx):
                source = (my_y - far) % self.ny * self.nx + (my_x - near) % self.nx
                block = jnp.concatenate([first[far][near], second[near][far]])
                out = lax.dynamic_update_index_in_dim(out, block, source, 0)
        return out

    def sum_all(self, value):
        step = 1
        while step < self.tensor:
            pairs = [(t, t ^ step) for t in range(self.tensor)]
            value = value + lax.ppermute(value, "tensor", pairs)
            step *= 2
        step = 1
        while step < self.dp:
            pairs = [(d, d ^ step) for d in range(self.dp)]
            value = value + lax.ppermute(value, "dp", pairs)
            step *= 2
        return value


def place(vector, index, total):
    row = jnp.zeros((total,), jnp.float32)
    return lax.dynamic_update_slice(row, vector.astype(jnp.float32), (index * vector.shape[0],))


def per_device(
    dp_size,
    tensor_size,
    inputs,
    project,
    offsets,
    combine,
    combine_bias,
    norm_gain,
    norm_shift,
    expand,
    expand_bias,
    contract,
    contract_bias,
    cotangent,
):
    plane = Plane(dp_size, tensor_size)
    levels = tensor_size // CORES
    same_core = [[z * CORES + core for z in range(levels)] for core in range(CORES)]
    width = inputs.shape[1]
    local_cols = project.shape[2]
    heads_here = local_cols // HEAD_DIM
    group_rows = SEQ_DEV * L
    dp_here, tensor_here = lax.axis_index("dp"), lax.axis_index("tensor")
    core_here = tensor_here % CORES
    hidden_here = expand.shape[1]
    piece = hidden_here // dp_size

    row_values = inputs.astype(jnp.float32)
    normed_one, back_one = jax.vjp(layer_norm, row_values, norm_gain[0], norm_shift[0])
    normed_full = lax.all_gather(normed_one.astype(jnp.bfloat16), "tensor", axis=0, tiled=True)

    expand_piece = lax.dynamic_slice_in_dim(expand, dp_here * piece, piece, 1).T
    contract_piece = lax.dynamic_slice_in_dim(contract, dp_here * piece, piece, 0)
    pieces = lax.all_gather(
        jnp.concatenate([expand_piece, contract_piece]),
        "tensor",
        axis=0,
        axis_index_groups=same_core,
    )
    expand_rows = pieces[:, :piece].reshape(levels * piece, width)
    contract_rows = pieces[:, piece:].reshape(levels * piece, width)
    bias_all = lax.all_gather(expand_bias, "tensor", axis=0, axis_index_groups=same_core)
    bias_here = lax.dynamic_slice_in_dim(bias_all, dp_here * piece, piece, 1).reshape(-1)
    combine_full = lax.all_gather(combine, "tensor", axis=0, tiled=True)
    grad_chunks = plane.gather_rows(cotangent)

    mapped = jnp.einsum("td,kde->tke", normed_full, project, preferred_element_type=jnp.float32)
    bias_rows = jnp.stack([offsets[0], jnp.zeros_like(offsets[0]), offsets[1]])
    mapped = (mapped + bias_rows[None]).astype(jnp.bfloat16)
    head_split = mapped.reshape(SEQ_DEV, L, 3, heads_here, HEAD_DIM)
    queries = head_split[:, :, 0]
    keys_all = head_split[:, :, 1]
    values_all = head_split[:, :, 2]
    attended, log_totals = attend_forward(queries, keys_all, values_all)
    attended = attended.reshape(group_rows, local_cols)
    attended_rows = lax.all_to_all(attended, "tensor", 0, 1, tiled=True)
    branch = jnp.dot(attended_rows, combine_full, preferred_element_type=jnp.float32)
    hidden = row_values + (branch + combine_bias)
    normed_two, back_two = jax.vjp(layer_norm, hidden, norm_gain[1], norm_shift[1])
    hidden_chunks = plane.gather_rows(normed_two.astype(jnp.bfloat16))

    mixed_chunks, active_chunks, before_grads, norm_grads = [], [], [], []
    for normed_part, grad_part in zip(hidden_chunks, grad_chunks):
        before = (
            jnp.einsum("td,fd->tf", normed_part, expand_rows, preferred_element_type=jnp.float32)
            + bias_here
        )
        active, gelu_back = jax.vjp(gelu_exact, before)
        active_low = active.astype(jnp.bfloat16)
        mixed_chunks.append(
            jnp.dot(active_low, contract_rows, preferred_element_type=jnp.float32).astype(
                jnp.bfloat16
            )
        )
        grad_active = jnp.einsum(
            "td,fd->tf", grad_part, contract_rows, preferred_element_type=jnp.float32
        )
        grad_before = gelu_back(grad_active)[0].astype(jnp.bfloat16)
        norm_grads.append(
            jnp.dot(grad_before, expand_rows, preferred_element_type=jnp.float32).astype(
                jnp.bfloat16
            )
        )
        active_chunks.append(active_low)
        before_grads.append(grad_before)
    grad_normed_two = plane.scatter_rows(norm_grads)
    grad_local = cotangent.astype(jnp.float32)
    grad_hidden_norm, gain_two_grad, shift_two_grad = back_two(grad_normed_two)
    grad_hidden = grad_local + grad_hidden_norm
    grad_branch = grad_hidden.astype(jnp.bfloat16)
    grad_attended_rows = jnp.einsum(
        "td,ed->te", grad_branch, combine_full, preferred_element_type=jnp.float32
    ).astype(jnp.bfloat16)
    grad_attended = lax.all_to_all(grad_attended_rows, "tensor", 1, 0, tiled=True)

    mixed = plane.scatter_rows(mixed_chunks)
    block_out = (hidden + mixed + contract_bias).astype(jnp.bfloat16)
    contract_part = jnp.zeros((levels * piece, width), jnp.float32)
    expand_part = jnp.zeros((levels * piece, width), jnp.float32)
    widening_part = jnp.zeros((levels * piece,), jnp.float32)
    for normed_part, grad_part, active_low, grad_before in zip(
        hidden_chunks, grad_chunks, active_chunks, before_grads
    ):
        contract_part += jnp.einsum(
            "tf,td->fd", active_low, grad_part, preferred_element_type=jnp.float32
        )
        expand_part += jnp.einsum(
            "tf,td->fd", grad_before, normed_part, preferred_element_type=jnp.float32
        )
        widening_part += jnp.sum(grad_before.astype(jnp.float32), axis=0)
    stacked = jnp.concatenate(
        [
            expand_part.reshape(levels, piece, width),
            contract_part.reshape(levels, piece, width),
        ],
        axis=1,
    ).astype(jnp.bfloat16)
    hidden_grads = lax.psum_scatter(
        stacked, "tensor", scatter_dimension=0, axis_index_groups=same_core
    )
    hidden_grads = plane.gather_dp(hidden_grads)
    expand_grad = hidden_grads[:, :piece].reshape(hidden_here, width).T.astype(jnp.float32)
    contract_grad = hidden_grads[:, piece:].reshape(hidden_here, width).astype(jnp.float32)
    combine_part = lax.psum_scatter(
        jnp.einsum(
            "te,td->ed", attended_rows, grad_branch, preferred_element_type=jnp.float32
        ).astype(jnp.bfloat16),
        "tensor",
        scatter_dimension=0,
        tiled=True,
    )

    query_grad, key_grad, value_grad = attend_backward(
        queries,
        keys_all,
        values_all,
        grad_attended.reshape(SEQ_DEV, L, heads_here, HEAD_DIM),
        log_totals,
    )
    grad_mapped = (
        jnp.stack([query_grad, key_grad, value_grad], axis=2)
        .reshape(group_rows, 3, local_cols)
        .astype(jnp.bfloat16)
    )
    grad_normed_one = lax.psum_scatter(
        jnp.einsum("tke,kde->td", grad_mapped, project, preferred_element_type=jnp.float32).astype(
            jnp.bfloat16
        ),
        "tensor",
        scatter_dimension=0,
        tiled=True,
    ).astype(jnp.float32)
    mapped_sums = jnp.sum(grad_mapped.astype(jnp.float32), axis=0)
    project_grad = jnp.einsum(
        "td,tke->kde", normed_full, grad_mapped, preferred_element_type=jnp.float32
    )
    project_wide = project.astype(jnp.float32)
    shift_one_grad = jnp.sum(project_wide * mapped_sums[:, None, :], axis=(0, 2))
    both_one = jnp.sum(project_wide * project_grad, axis=(0, 2))
    gain_one_grad = (both_one - norm_shift[0] * shift_one_grad) / norm_gain[0]

    widening_rows = jnp.stack(
        [
            place(
                widening_part.reshape(levels, piece)[z],
                (z * CORES + core_here) * dp_size + dp_here,
                tensor_size * hidden_here,
            )
            for z in range(levels)
        ]
    ).sum(axis=0)
    small = jnp.concatenate(
        [
            jnp.sum(grad_branch.astype(jnp.float32), axis=0),
            gain_one_grad,
            gain_two_grad,
            shift_one_grad,
            shift_two_grad,
            jnp.sum(grad_local, axis=0),
            place(mapped_sums[0], tensor_here, width),
            place(mapped_sums[2], tensor_here, width),
            widening_rows,
        ]
    ).reshape(-1, width)
    small = plane.sum_all(small)
    mixing_grad, narrowing_grad = small[0], small[5]
    gain_grad, shift_grad = small[1:3], small[3:5]
    offset_grad = lax.dynamic_slice_in_dim(small[6:8], tensor_here * local_cols, local_cols, 1)
    widening_grad = lax.dynamic_slice_in_dim(
        small[8:].reshape(-1), tensor_here * hidden_here, hidden_here, 0
    )

    attention_grads = jnp.concatenate(
        [project_grad.astype(jnp.bfloat16).reshape(-1, width), combine_part]
    )
    attention_grads = plane.sum_dp(attention_grads)
    project_rows = 3 * local_cols
    project_grad = attention_grads[:project_rows].reshape(project.shape)
    combine_grad = attention_grads[project_rows:]

    grad_input_norm, _, _ = back_one(grad_normed_one)
    input_grad = (grad_hidden + grad_input_norm).astype(jnp.bfloat16)
    return (
        block_out,
        input_grad,
        project_grad,
        offset_grad,
        combine_grad,
        mixing_grad,
        gain_grad,
        shift_grad,
        expand_grad,
        widening_grad,
        contract_grad,
        narrowing_grad,
    )


def solution(mesh):
    placed = (
        P(("dp", "tensor"), None),
        P(None, None, "tensor"),
        P(None, "tensor"),
        P("tensor", None),
        P(),
        P(),
        P(),
        P(None, "tensor"),
        P("tensor"),
        P("tensor", None),
        P(),
        P(("dp", "tensor"), None),
    )
    return jax.shard_map(
        functools.partial(per_device, mesh.shape["dp"], mesh.shape["tensor"]),
        mesh=mesh,
        in_specs=placed,
        out_specs=(
            P(("dp", "tensor"), None),
            P(("dp", "tensor"), None),
            P(None, None, "tensor"),
            P(None, "tensor"),
            P("tensor", None),
            P(),
            P(),
            P(),
            P(None, "tensor"),
            P("tensor"),
            P("tensor", None),
            P(),
        ),
        check_vma=False,
    )
```

```python
import functools
import math

import jax
import jax.numpy as jnp
from jax import lax
from jax.experimental import pallas as pl
from jax.experimental.pallas import tpu as pltpu
from jax.sharding import PartitionSpec as P

L = 2048
QBLOCK = 256
KCHUNK = 512
CORES = 2
HEAD_DIM = 64


def layer_norm(features, gain_row, shift_row):
    center = features - jnp.mean(features, axis=-1, keepdims=True)
    spread = jnp.mean(center * center, axis=-1, keepdims=True)
    return center * lax.rsqrt(spread + 1e-06) * gain_row + shift_row


def gelu_exact(values):
    return jax.nn.gelu(values, approximate=False)


INTERPRET = False


def heads_of(cols):
    lane = lax.broadcasted_iota(jnp.int32, (1, cols), 1)
    return [(lane >= h * HEAD_DIM) & (lane < (h + 1) * HEAD_DIM) for h in range(cols // HEAD_DIM)]


def dot_last(left, right):
    return lax.dot_general(left, right, (((1,), (1,)), ((), ())), preferred_element_type=jnp.float32)


def forward_kernel(cols, block, mapped_ref, out_ref, total_ref):
    step = pl.program_id(0)
    rows = pl.ds(pl.multiple_of(step * block, block), block)
    queries = mapped_ref[rows, :cols]
    keys = mapped_ref[:, cols : 2 * cols]
    values = mapped_ref[:, 2 * cols :].T
    scale = 1.0 / math.sqrt(HEAD_DIM)
    results = []
    for head, mask in enumerate(heads_of(cols)):
        query = jnp.where(mask, queries, jnp.zeros_like(queries))
        scores = dot_last(keys, query) * scale
        highest = jnp.max(scores, axis=0, keepdims=True)
        raised = jnp.exp(scores - highest)
        summed = jnp.sum(raised, axis=0, keepdims=True)
        result = jnp.dot(
            values[head * HEAD_DIM : (head + 1) * HEAD_DIM],
            raised.astype(jnp.bfloat16),
            preferred_element_type=jnp.float32,
        )
        results.append(result / summed)
        total_ref[head : head + 1, :] = highest + jnp.log(summed)
    out_ref[...] = jnp.concatenate(results, axis=0).T.astype(jnp.bfloat16)


def attend_forward(mapped, block):
    length, cols = mapped.shape[0], mapped.shape[1] // 3
    heads = cols // HEAD_DIM
    return pl.pallas_call(
        functools.partial(forward_kernel, cols, block),
        grid=(length // block,),
        in_specs=[pl.BlockSpec((length, 3 * cols), lambda i: (0, 0))],
        out_specs=[
            pl.BlockSpec((block, cols), lambda i: (i, 0)),
            pl.BlockSpec((heads, block), lambda i: (0, i)),
        ],
        out_shape=[
            jax.ShapeDtypeStruct((length, cols), jnp.bfloat16),
            jax.ShapeDtypeStruct((heads, length), jnp.float32),
        ],
        name="attend_forward",
        interpret=INTERPRET,
    )(mapped)


def backward_kernel(
    cols, block, chunk, mapped_ref, grad_ref, attended_ref, total_ref, out_ref, key_acc, value_acc
):
    step = pl.program_id(0)
    length = mapped_ref.shape[0]
    rows = pl.ds(pl.multiple_of(step * block, block), block)
    scale = 1.0 / math.sqrt(HEAD_DIM)

    @pl.when(step == 0)
    def _():
        key_acc[...] = jnp.zeros_like(key_acc)
        value_acc[...] = jnp.zeros_like(value_acc)

    queries = mapped_ref[rows, :cols]
    grads = grad_ref[...]
    products = (grads.astype(jnp.float32) * attended_ref[...].astype(jnp.float32)).T
    query_grads = []
    masks = heads_of(cols)
    parts = []
    for head, mask in enumerate(masks):
        dots = jnp.sum(products[head * HEAD_DIM : (head + 1) * HEAD_DIM], axis=0, keepdims=True)
        parts.append(
            (
                jnp.where(mask, queries, jnp.zeros_like(queries)),
                jnp.where(mask, grads, jnp.zeros_like(grads)),
                dots,
                total_ref[head : head + 1, :],
            )
        )
        query_grads.append(jnp.zeros((HEAD_DIM, block), jnp.float32))
    for begin in range(0, length, chunk):
        span = slice(begin, begin + chunk)
        keys = mapped_ref[span, cols : 2 * cols]
        values = mapped_ref[span, 2 * cols :]
        keys_turned = keys.T
        key_part = value_part = None
        for head, (query, grad, dots, total) in enumerate(parts):
            probs = jnp.exp(dot_last(keys, query) * scale - total)
            grad_scores = (probs * (dot_last(values, grad) - dots)).astype(jnp.bfloat16)
            query_grads[head] += jnp.dot(
                keys_turned[head * HEAD_DIM : (head + 1) * HEAD_DIM],
                grad_scores,
                preferred_element_type=jnp.float32,
            )
            key_here = jnp.dot(grad_scores, query, preferred_element_type=jnp.float32)
            value_here = jnp.dot(
                probs.astype(jnp.bfloat16), grad, preferred_element_type=jnp.float32
            )
            key_part = key_here if key_part is None else key_part + key_here
            value_part = value_here if value_part is None else value_part + value_here
        key_acc[span, :] += key_part
        value_acc[span, :] += value_part
    query_grad = jnp.concatenate(query_grads, axis=0).T * scale
    out_ref[rows, :cols] = query_grad.astype(jnp.bfloat16)

    @pl.when(step == pl.num_programs(0) - 1)
    def _():
        out_ref[:, cols : 2 * cols] = (key_acc[...] * scale).astype(jnp.bfloat16)
        out_ref[:, 2 * cols :] = value_acc[...].astype(jnp.bfloat16)


def attend_backward(mapped, grad_out, attended, log_totals, block, chunk):
    length, cols = grad_out.shape
    heads = cols // HEAD_DIM
    return pl.pallas_call(
        functools.partial(backward_kernel, cols, block, chunk),
        grid=(length // block,),
        in_specs=[
            pl.BlockSpec((length, 3 * cols), lambda i: (0, 0)),
            pl.BlockSpec((block, cols), lambda i: (i, 0)),
            pl.BlockSpec((block, cols), lambda i: (i, 0)),
            pl.BlockSpec((heads, block), lambda i: (0, i)),
        ],
        out_specs=pl.BlockSpec((length, 3 * cols), lambda i: (0, 0)),
        out_shape=jax.ShapeDtypeStruct((length, 3 * cols), jnp.bfloat16),
        scratch_shapes=[pltpu.VMEM((length, cols), jnp.float32)] * 2,
        name="attend_backward",
        interpret=INTERPRET,
    )(mapped, grad_out, attended, log_totals)


def grid_of(dp):
    nx = 1
    while nx * nx < dp:
        nx *= 2
    return dp // nx, nx


class Plane:
    def __init__(self, dp, tensor):
        self.ny, self.nx = grid_of(dp)
        self.dp, self.tensor = dp, tensor

    def _perm(self, axis, step):
        ny, nx = self.ny, self.nx
        if axis == "x":
            return [(y * nx + x, y * nx + (x + step) % nx) for y in range(ny) for x in range(nx)]
        return [(y * nx + x, (y + step) % ny * nx + x) for y in range(ny) for x in range(nx)]

    def size(self, axis):
        return self.nx if axis == "x" else self.ny

    def swap_cores(self, value):
        return lax.ppermute(value, "tensor", [(t, t ^ 1) for t in range(self.tensor)])

    def gather(self, value, axis):
        parts = [value]
        for _ in range(self.size(axis) - 1):
            parts.append(lax.ppermute(parts[-1], "dp", self._perm(axis, 1)))
        return parts

    def scatter(self, parts, axis):
        total = parts[-1]
        for part in parts[-2::-1]:
            moved = lax.ppermute(total.astype(jnp.bfloat16), "dp", self._perm(axis, -1))
            total = part + moved.astype(jnp.float32)
        return total

    def gather_rows(self, rows):
        half = rows.shape[0] // 2
        first, second = rows[:half], rows[half:]
        by_x = self.gather(first, "x")
        by_y = self.gather(second, "y")
        near = jnp.concatenate(by_x[1:] + by_y[1:])
        far_first = self.gather(jnp.concatenate(by_x), "y")[1:]
        far_second = self.gather(jnp.concatenate(by_y), "x")[1:]
        far = jnp.concatenate(far_first + far_second)
        return [jnp.concatenate([part, self.swap_cores(part)]) for part in (rows, near, far)]

    def scatter_rows(self, chunks):
        own, near, far = [self._fold(chunk) for chunk in chunks]
        half = own.shape[0] // 2
        size_x, size_y = half * self.nx, half * self.ny
        split = size_x * (self.ny - 1)
        far_first = [far[k * size_x : (k + 1) * size_x] for k in range(self.ny - 1)]
        far_second = [far[split + k * size_y : split + (k + 1) * size_y] for k in range(self.nx - 1)]
        near_first, near_second = near[: size_x - half], near[size_x - half :]
        first = self.scatter([jnp.concatenate([own[:half], near_first])] + far_first, "y")
        second = self.scatter([jnp.concatenate([own[half:], near_second])] + far_second, "x")
        first = self.scatter([first[k * half : (k + 1) * half] for k in range(self.nx)], "x")
        second = self.scatter([second[k * half : (k + 1) * half] for k in range(self.ny)], "y")
        return jnp.concatenate([first, second])

    def _fold(self, chunk):
        half = chunk.shape[0] // 2
        return chunk[:half].astype(jnp.float32) + self.swap_cores(chunk[half:]).astype(jnp.float32)

    def sum_dp(self, value):
        half = value.shape[0] // 2
        halves = []
        for part, axes in ((value[:half], "xy"), (value[half:], "yx")):
            for axis in axes:
                gathered = self.gather(part, axis)
                total = sum(item.astype(jnp.float32) for item in gathered)
                part = total.astype(jnp.bfloat16)
            halves.append(total)
        return jnp.concatenate(halves)

    def gather_dp(self, value):
        half = value.shape[0] // 2
        first = self.gather(value[:half], "x")
        second = self.gather(value[half:], "y")
        first = self.gather(jnp.stack(first), "y")
        second = self.gather(jnp.stack(second), "x")
        me = lax.axis_index("dp")
        my_y, my_x = me // self.nx, me % self.nx
        out = jnp.zeros((self.dp,) + value.shape, value.dtype)
        for far in range(self.ny):
            for near in range(self.nx):
                source = (my_y - far) % self.ny * self.nx + (my_x - near) % self.nx
                block = jnp.concatenate([first[far][near], second[near][far]])
                out = lax.dynamic_update_index_in_dim(out, block, source, 0)
        return out

    def sum_all(self, value):
        step = 1
        while step < self.tensor:
            pairs = [(t, t ^ step) for t in range(self.tensor)]
            value = value + lax.ppermute(value, "tensor", pairs)
            step *= 2
        step = 1
        while step < self.dp:
            pairs = [(d, d ^ step) for d in range(self.dp)]
            value = value + lax.ppermute(value, "dp", pairs)
            step *= 2
        return value


def place(vector, index, total):
    row = jnp.zeros((total,), jnp.float32)
    return lax.dynamic_update_slice(row, vector.astype(jnp.float32), (index * vector.shape[0],))


def per_device(
    dp_size,
    tensor_size,
    inputs,
    project,
    offsets,
    combine,
    combine_bias,
    norm_gain,
    norm_shift,
    expand,
    expand_bias,
    contract,
    contract_bias,
    cotangent,
):
    plane = Plane(dp_size, tensor_size)
    levels = tensor_size // CORES
    same_core = [[z * CORES + core for z in range(levels)] for core in range(CORES)]
    width = inputs.shape[1]
    local_cols = project.shape[2]
    dp_here, tensor_here = lax.axis_index("dp"), lax.axis_index("tensor")
    core_here = tensor_here % CORES
    hidden_here = expand.shape[1]
    piece = hidden_here // dp_size

    row_values = inputs.astype(jnp.float32)
    normed_one, back_one = jax.vjp(layer_norm, row_values, norm_gain[0], norm_shift[0])
    normed_full = lax.all_gather(normed_one.astype(jnp.bfloat16), "tensor", axis=0, tiled=True)

    expand_piece = lax.dynamic_slice_in_dim(expand, dp_here * piece, piece, 1).T
    contract_piece = lax.dynamic_slice_in_dim(contract, dp_here * piece, piece, 0)
    pieces = lax.all_gather(
        jnp.concatenate([expand_piece, contract_piece]),
        "tensor",
        axis=0,
        axis_index_groups=same_core,
    )
    expand_rows = pieces[:, :piece].reshape(levels * piece, width)
    contract_rows = pieces[:, piece:].reshape(levels * piece, width)
    bias_all = lax.all_gather(expand_bias, "tensor", axis=0, axis_index_groups=same_core)
    bias_here = lax.dynamic_slice_in_dim(bias_all, dp_here * piece, piece, 1).reshape(-1)
    combine_full = lax.all_gather(combine, "tensor", axis=0, tiled=True)
    grad_chunks = plane.gather_rows(cotangent)

    project_flat = project.transpose(1, 0, 2).reshape(width, 3 * local_cols)
    bias_row = jnp.concatenate([offsets[0], jnp.zeros_like(offsets[0]), offsets[1]])
    mapped = jnp.dot(normed_full, project_flat, preferred_element_type=jnp.float32) + bias_row
    mapped = mapped.astype(jnp.bfloat16)
    attended, log_totals = attend_forward(mapped, QBLOCK)
    attended_rows = lax.all_to_all(attended, "tensor", 0, 1, tiled=True)
    branch = jnp.dot(attended_rows, combine_full, preferred_element_type=jnp.float32)
    hidden = row_values + (branch + combine_bias)
    normed_two, back_two = jax.vjp(layer_norm, hidden, norm_gain[1], norm_shift[1])
    hidden_chunks = plane.gather_rows(normed_two.astype(jnp.bfloat16))

    mixed_chunks, active_chunks, before_grads, norm_grads = [], [], [], []
    for normed_part, grad_part in zip(hidden_chunks, grad_chunks):
        before = (
            jnp.einsum("td,fd->tf", normed_part, expand_rows, preferred_element_type=jnp.float32)
            + bias_here
        )
        active, gelu_back = jax.vjp(gelu_exact, before)
        active_low = active.astype(jnp.bfloat16)
        mixed_chunks.append(
            jnp.dot(active_low, contract_rows, preferred_element_type=jnp.float32).astype(
                jnp.bfloat16
            )
        )
        grad_active = jnp.einsum(
            "td,fd->tf", grad_part, contract_rows, preferred_element_type=jnp.float32
        )
        grad_before = gelu_back(grad_active)[0].astype(jnp.bfloat16)
        norm_grads.append(
            jnp.dot(grad_before, expand_rows, preferred_element_type=jnp.float32).astype(
                jnp.bfloat16
            )
        )
        active_chunks.append(active_low)
        before_grads.append(grad_before)
    grad_normed_two = plane.scatter_rows(norm_grads)
    grad_local = cotangent.astype(jnp.float32)
    grad_hidden_norm, gain_two_grad, shift_two_grad = back_two(grad_normed_two)
    grad_hidden = grad_local + grad_hidden_norm
    grad_branch = grad_hidden.astype(jnp.bfloat16)
    grad_attended_rows = jnp.einsum(
        "td,ed->te", grad_branch, combine_full, preferred_element_type=jnp.float32
    ).astype(jnp.bfloat16)
    mixed_chunks, grad_attended_rows = lax.optimization_barrier((mixed_chunks, grad_attended_rows))
    grad_attended = lax.all_to_all(grad_attended_rows, "tensor", 1, 0, tiled=True)
    mixed = plane.scatter_rows(mixed_chunks)
    block_out = (hidden + mixed + contract_bias).astype(jnp.bfloat16)
    contract_part = jnp.zeros((levels * piece, width), jnp.float32)
    expand_part = jnp.zeros((levels * piece, width), jnp.float32)
    widening_part = jnp.zeros((levels * piece,), jnp.float32)
    for normed_part, grad_part, active_low, grad_before in zip(
        hidden_chunks, grad_chunks, active_chunks, before_grads
    ):
        contract_part += jnp.einsum(
            "tf,td->fd", active_low, grad_part, preferred_element_type=jnp.float32
        )
        expand_part += jnp.einsum(
            "tf,td->fd", grad_before, normed_part, preferred_element_type=jnp.float32
        )
        widening_part += jnp.sum(grad_before.astype(jnp.float32), axis=0)
    stacked = jnp.concatenate(
        [
            expand_part.reshape(levels, piece, width),
            contract_part.reshape(levels, piece, width),
        ],
        axis=1,
    ).astype(jnp.bfloat16)
    hidden_grads = lax.psum_scatter(
        stacked, "tensor", scatter_dimension=0, axis_index_groups=same_core
    )
    hidden_grads = plane.gather_dp(hidden_grads)
    expand_grad = hidden_grads[:, :piece].reshape(hidden_here, width).T.astype(jnp.float32)
    contract_grad = hidden_grads[:, piece:].reshape(hidden_here, width).astype(jnp.float32)
    combine_part = lax.psum_scatter(
        jnp.einsum(
            "te,td->ed", attended_rows, grad_branch, preferred_element_type=jnp.float32
        ).astype(jnp.bfloat16),
        "tensor",
        scatter_dimension=0,
        tiled=True,
    )

    grad_mapped = attend_backward(mapped, grad_attended, attended, log_totals, QBLOCK, KCHUNK)
    grad_normed_one = lax.psum_scatter(
        dot_last(grad_mapped, project_flat).astype(jnp.bfloat16),
        "tensor",
        scatter_dimension=0,
        tiled=True,
    ).astype(jnp.float32)
    mapped_sums = jnp.sum(grad_mapped.astype(jnp.float32), axis=0)
    project_grad = jnp.einsum(
        "td,te->de", normed_full, grad_mapped, preferred_element_type=jnp.float32
    )
    project_wide = project_flat.astype(jnp.float32)
    shift_one_grad = jnp.sum(project_wide * mapped_sums[None, :], axis=1)
    both_one = jnp.sum(project_wide * project_grad, axis=1)
    gain_one_grad = (both_one - norm_shift[0] * shift_one_grad) / norm_gain[0]

    widening_rows = jnp.stack(
        [
            place(
                widening_part.reshape(levels, piece)[z],
                (z * CORES + core_here) * dp_size + dp_here,
                tensor_size * hidden_here,
            )
            for z in range(levels)
        ]
    ).sum(axis=0)
    small = jnp.concatenate(
        [
            jnp.sum(grad_branch.astype(jnp.float32), axis=0),
            gain_one_grad,
            gain_two_grad,
            shift_one_grad,
            shift_two_grad,
            jnp.sum(grad_local, axis=0),
            place(mapped_sums[:local_cols], tensor_here, width),
            place(mapped_sums[2 * local_cols :], tensor_here, width),
            widening_rows,
        ]
    ).reshape(-1, width)
    small = plane.sum_all(small)
    mixing_grad, narrowing_grad = small[0], small[5]
    gain_grad, shift_grad = small[1:3], small[3:5]
    offset_grad = lax.dynamic_slice_in_dim(small[6:8], tensor_here * local_cols, local_cols, 1)
    widening_grad = lax.dynamic_slice_in_dim(
        small[8:].reshape(-1), tensor_here * hidden_here, hidden_here, 0
    )

    attention_grads = jnp.concatenate(
        [
            project_grad.astype(jnp.bfloat16)
            .reshape(width, 3, local_cols)
            .transpose(1, 0, 2)
            .reshape(-1, width),
            combine_part,
        ]
    )
    attention_grads = plane.sum_dp(attention_grads)
    project_rows = 3 * local_cols
    project_grad = attention_grads[:project_rows].reshape(project.shape)
    combine_grad = attention_grads[project_rows:]

    grad_input_norm, _, _ = back_one(grad_normed_one)
    input_grad = (grad_hidden + grad_input_norm).astype(jnp.bfloat16)
    return (
        block_out,
        input_grad,
        project_grad,
        offset_grad,
        combine_grad,
        mixing_grad,
        gain_grad,
        shift_grad,
        expand_grad,
        widening_grad,
        contract_grad,
        narrowing_grad,
    )


def solution(mesh):
    placed = (
        P(("dp", "tensor"), None),
        P(None, None, "tensor"),
        P(None, "tensor"),
        P("tensor", None),
        P(),
        P(),
        P(),
        P(None, "tensor"),
        P("tensor"),
        P("tensor", None),
        P(),
        P(("dp", "tensor"), None),
    )
    return jax.shard_map(
        functools.partial(per_device, mesh.shape["dp"], mesh.shape["tensor"]),
        mesh=mesh,
        in_specs=placed,
        out_specs=(
            P(("dp", "tensor"), None),
            P(("dp", "tensor"), None),
            P(None, None, "tensor"),
            P(None, "tensor"),
            P("tensor", None),
            P(),
            P(),
            P(),
            P(None, "tensor"),
            P("tensor"),
            P("tensor", None),
            P(),
        ),
        check_vma=False,
    )
```

```python
import functools
import math

import jax
import jax.numpy as jnp
from jax import lax
from jax.experimental import pallas as pl
from jax.experimental.pallas import tpu as pltpu
from jax.sharding import PartitionSpec as P

L = 2048
QBLOCK = 256
KCHUNK = 512
CORES = 2
HEAD_DIM = 64


def layer_norm(features, gain_row, shift_row):
    center = features - jnp.mean(features, axis=-1, keepdims=True)
    spread = jnp.mean(center * center, axis=-1, keepdims=True)
    return center * lax.rsqrt(spread + 1e-06) * gain_row + shift_row


def gelu_exact(values):
    return jax.nn.gelu(values, approximate=False)


INTERPRET = False


def heads_of(cols):
    lane = lax.broadcasted_iota(jnp.int32, (1, cols), 1)
    return [(lane >= h * HEAD_DIM) & (lane < (h + 1) * HEAD_DIM) for h in range(cols // HEAD_DIM)]


def dot_last(left, right):
    return lax.dot_general(left, right, (((1,), (1,)), ((), ())), preferred_element_type=jnp.float32)


def forward_kernel(cols, block, mapped_ref, out_ref, total_ref):
    step = pl.program_id(0)
    rows = pl.ds(pl.multiple_of(step * block, block), block)
    queries = mapped_ref[rows, :cols]
    keys = mapped_ref[:, cols : 2 * cols]
    values = mapped_ref[:, 2 * cols :].T
    scale = 1.0 / math.sqrt(HEAD_DIM)
    results = []
    for head, mask in enumerate(heads_of(cols)):
        query = jnp.where(mask, queries, jnp.zeros_like(queries))
        scores = dot_last(keys, query) * scale
        highest = jnp.max(scores, axis=0, keepdims=True)
        raised = jnp.exp(scores - highest)
        summed = jnp.sum(raised, axis=0, keepdims=True)
        result = jnp.dot(
            values[head * HEAD_DIM : (head + 1) * HEAD_DIM],
            raised.astype(jnp.bfloat16),
            preferred_element_type=jnp.float32,
        )
        results.append(result / summed)
        total_ref[head : head + 1, :] = highest + jnp.log(summed)
    out_ref[...] = jnp.concatenate(results, axis=0).T.astype(jnp.bfloat16)


def attend_forward(mapped, block):
    length, cols = mapped.shape[0], mapped.shape[1] // 3
    heads = cols // HEAD_DIM
    return pl.pallas_call(
        functools.partial(forward_kernel, cols, block),
        grid=(length // block,),
        in_specs=[pl.BlockSpec((length, 3 * cols), lambda i: (0, 0))],
        out_specs=[
            pl.BlockSpec((block, cols), lambda i: (i, 0)),
            pl.BlockSpec((heads, block), lambda i: (0, i)),
        ],
        out_shape=[
            jax.ShapeDtypeStruct((length, cols), jnp.bfloat16),
            jax.ShapeDtypeStruct((heads, length), jnp.float32),
        ],
        name="attend_forward",
        interpret=INTERPRET,
    )(mapped)


def backward_kernel(cols, block, chunk, first, last, *refs):
    mapped_ref, grad_ref, attended_ref, total_ref = refs[:4]
    if first:
        query_ref, key_acc, value_acc = refs[4:]
    else:
        before_ref, key_in, value_in, out_ref, key_acc, value_acc = refs[4:]
    step = pl.program_id(0)
    length = mapped_ref.shape[0]
    offset = 0 if first else before_ref.shape[0]
    rows = pl.ds(pl.multiple_of(offset + step * block, block), block)
    scale = 1.0 / math.sqrt(HEAD_DIM)

    @pl.when(step == 0)
    def _():
        if first:
            key_acc[...] = jnp.zeros_like(key_acc)
            value_acc[...] = jnp.zeros_like(value_acc)
        else:
            key_acc[...] = key_in[...]
            value_acc[...] = value_in[...]
            out_ref[: before_ref.shape[0], :cols] = before_ref[...]

    queries = mapped_ref[rows, :cols]
    grads = grad_ref[...]
    products = (grads.astype(jnp.float32) * attended_ref[...].astype(jnp.float32)).T
    query_grads = []
    parts = []
    for head, mask in enumerate(heads_of(cols)):
        dots = jnp.sum(products[head * HEAD_DIM : (head + 1) * HEAD_DIM], axis=0, keepdims=True)
        parts.append(
            (
                jnp.where(mask, queries, jnp.zeros_like(queries)),
                jnp.where(mask, grads, jnp.zeros_like(grads)),
                dots,
                total_ref[head : head + 1, :],
            )
        )
        query_grads.append(jnp.zeros((HEAD_DIM, block), jnp.float32))
    for begin in range(0, length, chunk):
        span = slice(begin, begin + chunk)
        keys = mapped_ref[span, cols : 2 * cols]
        values = mapped_ref[span, 2 * cols :]
        keys_turned = keys.T
        key_part = value_part = None
        for head, (query, grad, dots, total) in enumerate(parts):
            probs = jnp.exp(dot_last(keys, query) * scale - total)
            grad_scores = (probs * (dot_last(values, grad) - dots)).astype(jnp.bfloat16)
            query_grads[head] += jnp.dot(
                keys_turned[head * HEAD_DIM : (head + 1) * HEAD_DIM],
                grad_scores,
                preferred_element_type=jnp.float32,
            )
            key_here = jnp.dot(grad_scores, query, preferred_element_type=jnp.float32)
            value_here = jnp.dot(
                probs.astype(jnp.bfloat16), grad, preferred_element_type=jnp.float32
            )
            key_part = key_here if key_part is None else key_part + key_here
            value_part = value_here if value_part is None else value_part + value_here
        key_acc[span, :] += key_part
        value_acc[span, :] += value_part
    query_grad = (jnp.concatenate(query_grads, axis=0).T * scale).astype(jnp.bfloat16)
    if first:
        query_ref[...] = query_grad
    else:
        out_ref[rows, :cols] = query_grad

    if last:

        @pl.when(step == pl.num_programs(0) - 1)
        def _():
            out_ref[:, cols : 2 * cols] = (key_acc[...] * scale).astype(jnp.bfloat16)
            out_ref[:, 2 * cols :] = value_acc[...].astype(jnp.bfloat16)


def attend_backward(mapped, grad_out, attended, log_totals, block, chunk, carried=None):
    length, cols = grad_out.shape
    heads = cols // HEAD_DIM
    steps = length // block // 2
    shift = 0 if carried is None else steps
    whole = pl.BlockSpec((length, cols), lambda i: (0, 0))
    in_specs = [
        pl.BlockSpec((length, 3 * cols), lambda i: (0, 0)),
        pl.BlockSpec((block, cols), lambda i: (i + shift, 0)),
        pl.BlockSpec((block, cols), lambda i: (i + shift, 0)),
        pl.BlockSpec((heads, block), lambda i: (0, i + shift)),
    ]
    sums = jax.ShapeDtypeStruct((length, cols), jnp.float32)
    if carried is None:
        out_specs = [pl.BlockSpec((block, cols), lambda i: (i, 0)), whole, whole]
        out_shape = [jax.ShapeDtypeStruct((length // 2, cols), jnp.bfloat16), sums, sums]
        scratch = []
        extra = ()
    else:
        in_specs += [pl.BlockSpec((length // 2, cols), lambda i: (0, 0)), whole, whole]
        out_specs = pl.BlockSpec((length, 3 * cols), lambda i: (0, 0))
        out_shape = jax.ShapeDtypeStruct((length, 3 * cols), jnp.bfloat16)
        scratch = [pltpu.VMEM((length, cols), jnp.float32)] * 2
        extra = tuple(carried)
    first = carried is None
    return pl.pallas_call(
        functools.partial(backward_kernel, cols, block, chunk, first, not first),
        grid=(steps,),
        in_specs=in_specs,
        out_specs=out_specs,
        out_shape=out_shape,
        scratch_shapes=scratch,
        name="attend_backward_a" if first else "attend_backward_b",
        interpret=INTERPRET,
    )(mapped, grad_out, attended, log_totals, *extra)


def grid_of(dp):
    nx = 1
    while nx * nx < dp:
        nx *= 2
    return dp // nx, nx


class Plane:
    def __init__(self, dp, tensor):
        self.ny, self.nx = grid_of(dp)
        self.dp, self.tensor = dp, tensor

    def _perm(self, axis, step):
        ny, nx = self.ny, self.nx
        if axis == "x":
            return [(y * nx + x, y * nx + (x + step) % nx) for y in range(ny) for x in range(nx)]
        return [(y * nx + x, (y + step) % ny * nx + x) for y in range(ny) for x in range(nx)]

    def size(self, axis):
        return self.nx if axis == "x" else self.ny

    def swap_cores(self, value):
        return lax.ppermute(value, "tensor", [(t, t ^ 1) for t in range(self.tensor)])

    def gather(self, value, axis):
        parts = [value]
        for _ in range(self.size(axis) - 1):
            parts.append(lax.ppermute(parts[-1], "dp", self._perm(axis, 1)))
        return parts

    def scatter(self, parts, axis):
        total = parts[-1]
        for part in parts[-2::-1]:
            moved = lax.ppermute(total.astype(jnp.bfloat16), "dp", self._perm(axis, -1))
            total = part + moved.astype(jnp.float32)
        return total

    def gather_rows(self, rows):
        half = rows.shape[0] // 2
        first, second = rows[:half], rows[half:]
        by_x = self.gather(first, "x")
        by_y = self.gather(second, "y")
        near = jnp.concatenate(by_x[1:] + by_y[1:])
        far_first = self.gather(jnp.concatenate(by_x), "y")[1:]
        far_second = self.gather(jnp.concatenate(by_y), "x")[1:]
        far = jnp.concatenate(far_first + far_second)
        return [jnp.concatenate([part, self.swap_cores(part)]) for part in (rows, near, far)]

    def scatter_rows(self, chunks):
        own, near, far = [self._fold(chunk) for chunk in chunks]
        half = own.shape[0] // 2
        size_x, size_y = half * self.nx, half * self.ny
        split = size_x * (self.ny - 1)
        far_first = [far[k * size_x : (k + 1) * size_x] for k in range(self.ny - 1)]
        far_second = [far[split + k * size_y : split + (k + 1) * size_y] for k in range(self.nx - 1)]
        near_first, near_second = near[: size_x - half], near[size_x - half :]
        first = self.scatter([jnp.concatenate([own[:half], near_first])] + far_first, "y")
        second = self.scatter([jnp.concatenate([own[half:], near_second])] + far_second, "x")
        first = self.scatter([first[k * half : (k + 1) * half] for k in range(self.nx)], "x")
        second = self.scatter([second[k * half : (k + 1) * half] for k in range(self.ny)], "y")
        return jnp.concatenate([first, second])

    def _fold(self, chunk):
        half = chunk.shape[0] // 2
        return chunk[:half].astype(jnp.float32) + self.swap_cores(chunk[half:]).astype(jnp.float32)

    def sum_dp(self, value):
        half = value.shape[0] // 2
        halves = []
        for part, axes in ((value[:half], "xy"), (value[half:], "yx")):
            for axis in axes:
                gathered = self.gather(part, axis)
                total = sum(item.astype(jnp.float32) for item in gathered)
                part = total.astype(jnp.bfloat16)
            halves.append(total)
        return jnp.concatenate(halves)

    def gather_dp_near(self, value):
        half = value.shape[0] // 2
        first = self.gather(value[:half], "x")
        second = self.gather(value[half:], "y")
        return jnp.stack(first), jnp.stack(second)

    def gather_dp_far(self, near):
        first, second = near
        return jnp.stack(self.gather(first, "y")), jnp.stack(self.gather(second, "x"))

    def order_dp(self, far):
        first, second = far
        me = lax.axis_index("dp")
        my_y, my_x = me // self.nx, me % self.nx
        half = first.shape[2]
        out = jnp.zeros((self.dp, 2 * half) + first.shape[3:], first.dtype)
        for far in range(self.ny):
            for near in range(self.nx):
                source = (my_y - far) % self.ny * self.nx + (my_x - near) % self.nx
                block = jnp.concatenate([first[far, near], second[near, far]])
                out = lax.dynamic_update_index_in_dim(out, block, source, 0)
        return out

    def sum_all(self, value):
        step = 1
        while step < self.tensor:
            pairs = [(t, t ^ step) for t in range(self.tensor)]
            value = value + lax.ppermute(value, "tensor", pairs)
            step *= 2
        step = 1
        while step < self.dp:
            pairs = [(d, d ^ step) for d in range(self.dp)]
            value = value + lax.ppermute(value, "dp", pairs)
            step *= 2
        return value


def place(vector, index, total):
    row = jnp.zeros((total,), jnp.float32)
    return lax.dynamic_update_slice(row, vector.astype(jnp.float32), (index * vector.shape[0],))


def per_device(
    dp_size,
    tensor_size,
    inputs,
    project,
    offsets,
    combine,
    combine_bias,
    norm_gain,
    norm_shift,
    expand,
    expand_bias,
    contract,
    contract_bias,
    cotangent,
):
    plane = Plane(dp_size, tensor_size)
    levels = tensor_size // CORES
    same_core = [[z * CORES + core for z in range(levels)] for core in range(CORES)]
    width = inputs.shape[1]
    local_cols = project.shape[2]
    dp_here, tensor_here = lax.axis_index("dp"), lax.axis_index("tensor")
    core_here = tensor_here % CORES
    hidden_here = expand.shape[1]
    piece = hidden_here // dp_size

    row_values = inputs.astype(jnp.float32)
    normed_one, back_one = jax.vjp(layer_norm, row_values, norm_gain[0], norm_shift[0])
    normed_full = lax.all_gather(normed_one.astype(jnp.bfloat16), "tensor", axis=0, tiled=True)

    expand_piece = lax.dynamic_slice_in_dim(expand, dp_here * piece, piece, 1).T
    contract_piece = lax.dynamic_slice_in_dim(contract, dp_here * piece, piece, 0)
    pieces = lax.all_gather(
        jnp.concatenate([expand_piece, contract_piece]),
        "tensor",
        axis=0,
        axis_index_groups=same_core,
    )
    expand_rows = pieces[:, :piece].reshape(levels * piece, width)
    contract_rows = pieces[:, piece:].reshape(levels * piece, width)
    bias_all = lax.all_gather(expand_bias, "tensor", axis=0, axis_index_groups=same_core)
    bias_here = lax.dynamic_slice_in_dim(bias_all, dp_here * piece, piece, 1).reshape(-1)
    combine_full = lax.all_gather(combine, "tensor", axis=0, tiled=True)
    grad_chunks = plane.gather_rows(cotangent)

    project_rows = project.transpose(0, 2, 1).reshape(3 * local_cols, width)
    bias_row = jnp.concatenate([offsets[0], jnp.zeros_like(offsets[0]), offsets[1]])
    mapped = (dot_last(normed_full, project_rows) + bias_row).astype(jnp.bfloat16)
    attended, log_totals = attend_forward(mapped, QBLOCK)
    attended_rows = lax.all_to_all(attended, "tensor", 0, 1, tiled=True)
    branch = jnp.dot(attended_rows, combine_full, preferred_element_type=jnp.float32)
    hidden = row_values + (branch + combine_bias)
    normed_two, back_two = jax.vjp(layer_norm, hidden, norm_gain[1], norm_shift[1])
    hidden_chunks = plane.gather_rows(normed_two.astype(jnp.bfloat16))

    mixed_chunks, active_chunks, before_grads, norm_grads = [], [], [], []
    for normed_part, grad_part in zip(hidden_chunks, grad_chunks):
        before = (
            jnp.einsum("td,fd->tf", normed_part, expand_rows, preferred_element_type=jnp.float32)
            + bias_here
        )
        active, gelu_back = jax.vjp(gelu_exact, before)
        active_low = active.astype(jnp.bfloat16)
        mixed_chunks.append(
            jnp.dot(active_low, contract_rows, preferred_element_type=jnp.float32).astype(
                jnp.bfloat16
            )
        )
        grad_active = jnp.einsum(
            "td,fd->tf", grad_part, contract_rows, preferred_element_type=jnp.float32
        )
        grad_before = gelu_back(grad_active)[0].astype(jnp.bfloat16)
        norm_grads.append(
            jnp.dot(grad_before, expand_rows, preferred_element_type=jnp.float32).astype(
                jnp.bfloat16
            )
        )
        active_chunks.append(active_low)
        before_grads.append(grad_before)
    grad_normed_two = plane.scatter_rows(norm_grads)
    grad_local = cotangent.astype(jnp.float32)
    grad_hidden_norm, gain_two_grad, shift_two_grad = back_two(grad_normed_two)
    grad_hidden = grad_local + grad_hidden_norm
    grad_branch = grad_hidden.astype(jnp.bfloat16)
    grad_attended_rows = jnp.einsum(
        "td,ed->te", grad_branch, combine_full, preferred_element_type=jnp.float32
    ).astype(jnp.bfloat16)
    mixed_chunks, grad_attended_rows = lax.optimization_barrier((mixed_chunks, grad_attended_rows))
    grad_attended = lax.all_to_all(grad_attended_rows, "tensor", 1, 0, tiled=True)
    mixed = plane.scatter_rows(mixed_chunks)
    contract_part = jnp.zeros((levels * piece, width), jnp.float32)
    expand_part = jnp.zeros((levels * piece, width), jnp.float32)
    widening_part = jnp.zeros((levels * piece,), jnp.float32)
    for normed_part, grad_part, active_low, grad_before in zip(
        hidden_chunks, grad_chunks, active_chunks, before_grads
    ):
        contract_part += jnp.einsum(
            "tf,td->fd", active_low, grad_part, preferred_element_type=jnp.float32
        )
        expand_part += jnp.einsum(
            "tf,td->fd", grad_before, normed_part, preferred_element_type=jnp.float32
        )
        widening_part += jnp.sum(grad_before.astype(jnp.float32), axis=0)
    stacked = jnp.concatenate(
        [
            expand_part.reshape(levels, piece, width),
            contract_part.reshape(levels, piece, width),
        ],
        axis=1,
    ).astype(jnp.bfloat16)
    hidden_grads = lax.psum_scatter(
        stacked, "tensor", scatter_dimension=0, axis_index_groups=same_core
    )
    hidden_near = plane.gather_dp_near(hidden_grads)
    combine_part = lax.psum_scatter(
        jnp.einsum(
            "te,td->ed", attended_rows, grad_branch, preferred_element_type=jnp.float32
        ).astype(jnp.bfloat16),
        "tensor",
        scatter_dimension=0,
        tiled=True,
    )

    grad_attended, mixed, hidden_near = lax.optimization_barrier((grad_attended, mixed, hidden_near))
    block_out = (hidden + mixed + contract_bias).astype(jnp.bfloat16)
    hidden_far = plane.gather_dp_far(hidden_near)
    attention_args = (mapped, grad_attended, attended, log_totals, QBLOCK, KCHUNK)
    carried = attend_backward(*attention_args)
    carried, hidden_far = lax.optimization_barrier((carried, hidden_far))
    grad_mapped = attend_backward(*attention_args, carried=carried)
    hidden_grads = plane.order_dp(hidden_far)
    expand_grad = hidden_grads[:, :piece].reshape(hidden_here, width).T.astype(jnp.float32)
    contract_grad = hidden_grads[:, piece:].reshape(hidden_here, width).astype(jnp.float32)
    grad_normed_one = lax.psum_scatter(
        jnp.dot(grad_mapped, project_rows, preferred_element_type=jnp.float32).astype(jnp.bfloat16),
        "tensor",
        scatter_dimension=0,
        tiled=True,
    ).astype(jnp.float32)
    mapped_sums = jnp.sum(grad_mapped.astype(jnp.float32), axis=0)
    project_grad = jnp.einsum(
        "te,td->ed", grad_mapped, normed_full, preferred_element_type=jnp.float32
    )
    project_wide = project_rows.astype(jnp.float32)
    shift_one_grad = jnp.sum(project_wide * mapped_sums[:, None], axis=0)
    both_one = jnp.sum(project_wide * project_grad, axis=0)
    gain_one_grad = (both_one - norm_shift[0] * shift_one_grad) / norm_gain[0]

    widening_rows = jnp.stack(
        [
            place(
                widening_part.reshape(levels, piece)[z],
                (z * CORES + core_here) * dp_size + dp_here,
                tensor_size * hidden_here,
            )
            for z in range(levels)
        ]
    ).sum(axis=0)
    small = jnp.concatenate(
        [
            jnp.sum(grad_branch.astype(jnp.float32), axis=0),
            gain_one_grad,
            gain_two_grad,
            shift_one_grad,
            shift_two_grad,
            jnp.sum(grad_local, axis=0),
            place(mapped_sums[:local_cols], tensor_here, width),
            place(mapped_sums[2 * local_cols :], tensor_here, width),
            widening_rows,
        ]
    ).reshape(-1, width)
    small = plane.sum_all(small)
    attention_grads = jnp.concatenate(
        [project_grad.astype(jnp.bfloat16), combine_part]
    )
    attention_grads = plane.sum_dp(attention_grads)
    grad_normed_one, small, attention_grads = lax.optimization_barrier(
        (grad_normed_one, small, attention_grads)
    )
    mixing_grad, narrowing_grad = small[0], small[5]
    gain_grad, shift_grad = small[1:3], small[3:5]
    offset_grad = lax.dynamic_slice_in_dim(small[6:8], tensor_here * local_cols, local_cols, 1)
    widening_grad = lax.dynamic_slice_in_dim(
        small[8:].reshape(-1), tensor_here * hidden_here, hidden_here, 0
    )
    project_grad = attention_grads[: 3 * local_cols].reshape(3, local_cols, width).transpose(0, 2, 1)
    combine_grad = attention_grads[3 * local_cols :]

    grad_input_norm, _, _ = back_one(grad_normed_one)
    input_grad = (grad_hidden + grad_input_norm).astype(jnp.bfloat16)
    return (
        block_out,
        input_grad,
        project_grad,
        offset_grad,
        combine_grad,
        mixing_grad,
        gain_grad,
        shift_grad,
        expand_grad,
        widening_grad,
        contract_grad,
        narrowing_grad,
    )


def solution(mesh):
    placed = (
        P(("dp", "tensor"), None),
        P(None, None, "tensor"),
        P(None, "tensor"),
        P("tensor", None),
        P(),
        P(),
        P(),
        P(None, "tensor"),
        P("tensor"),
        P("tensor", None),
        P(),
        P(("dp", "tensor"), None),
    )
    return jax.shard_map(
        functools.partial(per_device, mesh.shape["dp"], mesh.shape["tensor"]),
        mesh=mesh,
        in_specs=placed,
        out_specs=(
            P(("dp", "tensor"), None),
            P(("dp", "tensor"), None),
            P(None, None, "tensor"),
            P(None, "tensor"),
            P("tensor", None),
            P(),
            P(),
            P(),
            P(None, "tensor"),
            P("tensor"),
            P("tensor", None),
            P(),
        ),
        check_vma=False,
    )
```
